32 devices in a mesh: space: 8 (over y, x, core), rank: 4 (over z).
Axes of the slice: x: 2, y: 2, z: 4, core: 2. Of those that a mesh axis runs over, the one named last changes fastest.
Arguments:
- xfactor: float32 [128, 131072], P('rank', 'space'), may hold values from -6 to 6
- volume: float32 [3, 64, 64], replicated, may hold values from -0.75 to 0.75
- upwind: float32 [3, 64, 64], replicated, may hold values from -0.75 to 0.75
- neighbor: int32 [3, 2048], P(None, 'space'), may hold values from -1 to 2046, as said below
- coeffs: float32 [512, 128], replicated, may hold values from -0.25 to 0.25
Outputs:
- new_factor: float32 [128, 131072], P(None, ('space', 'rank'))
- r_factor: float32 [512, 512], replicated
The draws below stay inside these ranges and needn't reach their ends.
Inputs may be any that keep to these rules, and one draw needn't show every extreme that they name: neighbor[d, e] is -1 or an element between e - 32 and e - 1; the distance 32 occurs in every direction.
All inputs are finite; a program needn't handle non-finite values.
Results may differ from the reference program's by a relative error of at most 0.0001.
Values sent between devices are 32-bit elements; how exact they have to be, the bound alone decides.
A program may use at most 128 MiB of HBM per device.

```python
import jax
import jax.numpy as jnp
from jax import lax

NODES = 64
R = 128
HALO_EL = 32
NEL = 2048
NX = 131072
CAND = 512
COLS_DEV = 32


def draw_neighbor(key, part):
    offsets = jax.random.randint(key, (3, NEL), 1, HALO_EL + 1)
    offsets = offsets.at[:, NEL - 1].set(1)
    offsets = offsets.at[:, NEL - 2].set(HALO_EL)
    elements = jnp.arange(NEL, dtype=jnp.int32)[None, :]
    target = elements - offsets
    return jnp.where(target >= 0, target, -1).astype(jnp.int32)


def block_levels(own_key, dims, split, low, largest):
    factor_of, own = 1.0, jax.random.fold_in(own_key, 6)
    for axis_at, blocks in split:
        draws = jnp.exp(jax.random.uniform(jax.random.fold_in(own, axis_at), (blocks,), jnp.float32, low / len(split), largest / len(split)))
        factor_of = factor_of * jnp.repeat(draws, dims[axis_at] // blocks).reshape([-1 if axis == axis_at else 1 for axis in range(len(dims))])
    return factor_of


def gaussian(key, dims, deviation, limit, pieces=(), held_as=jnp.bfloat16):
    values = jax.random.normal(key, dims, jnp.float32) * deviation
    if len(pieces) > 0:
        values = block_levels(key, dims, pieces, -0.22, 0.18) * values
    return jnp.clip(values, min=-limit, max=limit).astype(held_as)


def setup_inputs(seed: int = 0) -> dict:
    streams_of = jax.random.split(jax.random.key(seed), 6)
    xfactor = gaussian(streams_of[0], (R, NX), 1.0, 6.0, ((0, 4), (1, 8)), jnp.float32)
    volume = gaussian(streams_of[1], (3, NODES, NODES), NODES ** -0.5, 0.75, (), jnp.float32)
    upwind = gaussian(streams_of[2], (3, NODES, NODES), NODES ** -0.5, 0.75, (), jnp.float32)
    neighbor = draw_neighbor(jax.random.fold_in(streams_of[5], 71), 0)
    coeffs = gaussian(streams_of[4], (CAND, R), CAND ** -0.5, 0.25, (), jnp.float32)
    return {"xfactor": xfactor, "volume": volume, "upwind": upwind, "neighbor": neighbor, "coeffs": coeffs}


def moved_all(xfactor, volume, upwind, neighbor):
    blocks = xfactor.reshape(R, NEL, NODES)
    result = []
    for direc in range(3):
        valid = neighbor[direc] >= 0
        index = jnp.where(valid, neighbor[direc], 0).astype(jnp.int32)
        neigh = jnp.take(blocks, index, axis=1) * valid.astype(jnp.float32)[None, :, None]
        here = jnp.einsum('ij,cej->cei', volume[direc], blocks, precision=lax.Precision.HIGHEST)
        there = jnp.einsum('ij,cej->cei', upwind[direc], neigh, precision=lax.Precision.HIGHEST)
        result.append((here + there).reshape(R, NX))
    return result

def reference(xfactor, volume, upwind, neighbor, coeffs):
    moved = moved_all(xfactor, volume, upwind, neighbor)
    stacked = jnp.stack([xfactor] + moved, axis=0)
    quarters = R // COLS_DEV
    stacked = stacked.reshape(4, quarters, COLS_DEV, NX)
    candidate = jnp.transpose(stacked, (1, 0, 2, 3)).reshape(CAND, NX)
    gram = jnp.dot(candidate, candidate.T, precision=lax.Precision.HIGHEST) / NX
    lower = jnp.linalg.cholesky(gram)
    basis = jax.scipy.linalg.solve_triangular(lower, candidate, lower=True)
    new_factor = jnp.dot(coeffs.T, basis, precision=lax.Precision.HIGHEST)
    return (new_factor, lower.T)
```

```python
import functools

import jax
import jax.numpy as jnp
from jax import lax
from jax.experimental import pallas as pl
from jax.experimental.pallas import tpu as pltpu
from jax.sharding import PartitionSpec as P

HALO_EL = 32
LANES = 128
MESH = pl.DeviceIdType.MESH
HIGHEST = lax.Precision.HIGHEST
F32, BF16 = jnp.float32, jnp.bfloat16
NT = (((1,), (1,)), ((), ()))
TN = (((0,), (0,)), ((), ()))
VMEM_LIMIT = 60 * 1024 * 1024


def split(value):
    high = value.astype(BF16)
    return high, (value - high.astype(F32)).astype(BF16)


def mm(a, b):
    return jnp.dot(a, b, preferred_element_type=F32)


def shifted(value, axis, steps):
    count = lax.axis_size(axis)
    first, last = (max(0, -steps), min(count, count - steps))
    return lax.ppermute(value, axis, [(source, source + steps) for source in range(first, last)])


def transport_kernel(dims, idx_ref, head_ref, body_ref, w_ref, *refs):
    cols, head_pairs, pairs, body_at, group, ranks, blocks, total_rows, more = dims
    if more:
        prev_ref, *refs = refs
    chi_ref, clo_ref, gram_ref, thi, tlo, lhi, llo, whi, wlo = refs
    tiles = head_pairs + pairs
    per = cols // ranks

    def fill(source, at, tile):
        value = source[:, pl.ds(pl.multiple_of(at * LANES, LANES), LANES)]
        thi[0, tile], tlo[0, tile] = split(value)
        thi[1, tile], tlo[1, tile] = split(pltpu.roll(value, LANES // 2, 1))

    @pl.loop(0, head_pairs)
    def _(pair):
        fill(head_ref, pair, pair)

    @pl.loop(0, pairs)
    def _(pair):
        fill(body_ref, body_at + pair, head_pairs + pair)

    zero = jnp.zeros((cols, LANES), BF16)
    for phase in range(2):
        thi[phase, tiles] = zero
        tlo[phase, tiles] = zero
    whi[...], wlo[...] = split(w_ref[...])
    left = lax.broadcasted_iota(jnp.int32, (cols, LANES), 1) < LANES // 2

    @pl.loop(0, pairs // group)
    def _(step):
        @pl.loop(0, group)
        def _(local):
            pair = step * group + local
            rows = pl.ds(pl.multiple_of(local * cols, cols), cols)
            for odd in range(2):
                near = [idx_ref[direc, 2 * pair + odd] for direc in range(3)]
                for table, out in ((thi, lhi), (tlo, llo)):
                    here = table[odd, head_pairs + pair]
                    first = table[1 - near[0] % 2, near[0] // 2]
                    second = table[near[1] % 2, near[1] // 2]
                    third = table[1 - near[2] % 2, near[2] // 2]
                    out[rows, odd * 256 : odd * 256 + 128] = jnp.where(left, here, first)
                    out[rows, odd * 256 + 128 : odd * 256 + 256] = jnp.where(left, second, third)

        moved = mm(lhi[...], whi[...]) + mm(llo[...], whi[...]) + mm(lhi[...], wlo[...])
        for local in range(group):
            pair = step * group + local
            lanes = pl.ds(pl.multiple_of(pair * LANES, LANES), LANES)
            for direc in range(3):
                high, low = split(moved[local * cols : (local + 1) * cols, direc * LANES : (direc + 1) * LANES])
                for quarter in range(ranks):
                    start = (4 * quarter + direc + 1) * per
                    chi_ref[start : start + per, lanes] = high[quarter * per : (quarter + 1) * per]
                    clo_ref[start : start + per, lanes] = low[quarter * per : (quarter + 1) * per]
            for quarter in range(ranks):
                part = slice(quarter * per, (quarter + 1) * per)
                chi_ref[4 * quarter * per : (4 * quarter + 1) * per, lanes] = thi[0, head_pairs + pair, part, :]
                clo_ref[4 * quarter * per : (4 * quarter + 1) * per, lanes] = tlo[0, head_pairs + pair, part, :]

    def product(a, b, row, col):
        return lax.dot_general(
            a[row * 128 : (row + 2) * 128, :], b[col * 128 : (col + 2) * 128, :], NT, preferred_element_type=F32
        )

    spots = [(row, col) for row in range(blocks) for col in range(row, blocks)]
    for row in range(0, blocks, 2):
        for col in range(row, blocks, 2):
            value = product(chi_ref, chi_ref, row, col) + product(chi_ref, clo_ref, row, col)
            value = (value + product(clo_ref, chi_ref, row, col)) / total_rows
            for r in range(2):
                for c in range(2):
                    if row + r <= col + c:
                        at = spots.index((row + r, col + c)) * 128
                        block = value[r * 128 : (r + 1) * 128, c * 128 : (c + 1) * 128]
                        if more:
                            block = block + prev_ref[at : at + 128, :]
                        gram_ref[at : at + 128, :] = block


def reduce_kernel(plan, in_ref, out_ref, acc, recv, zrecv, send_sem, recv_sem):
    halvings, doublings, ranks, rows = plan
    space, rank = lax.axis_index("space"), lax.axis_index("rank")

    def across(bit):
        return space + (1 - 2 * ((space // 2**bit) % 2)) * 2**bit

    barrier = pltpu.get_barrier_semaphore()
    for bit in range(halvings + doublings):
        pl.semaphore_signal(barrier, inc=1, device_id=(across(bit), rank), device_id_type=MESH)
    for step in range(1, ranks):
        pl.semaphore_signal(barrier, inc=1, device_id=(space, (rank + step) % ranks), device_id_type=MESH)
    pl.semaphore_wait(barrier, halvings + doublings + ranks - 1)

    used = [0]

    def send(src, dst, where):
        at = used[0]
        used[0] += 1
        copy = pltpu.make_async_remote_copy(
            src_ref=src, dst_ref=dst, send_sem=send_sem.at[at], recv_sem=recv_sem.at[at],
            device_id=where, device_id_type=MESH,
        )
        copy.start()
        return copy

    def window(ref, start, size):
        return ref.at[pl.ds(pl.multiple_of(start, 8), size), :]

    base, size, slot = 0, rows, 0
    bases = []
    for bit in range(halvings):
        half = size // 2
        mine = (space // 2**bit) % 2
        source = in_ref if bit == 0 else acc
        send(window(source, base + (1 - mine) * half, half), window(recv, slot, half), (across(bit), rank)).wait()
        bases.append((base, size))
        base = base + mine * half
        acc[pl.ds(pl.multiple_of(base, 8), half), :] = (
            source[pl.ds(pl.multiple_of(base, 8), half), :] + recv[slot : slot + half, :]
        )
        slot, size = slot + half, half
    piece = size // ranks
    copies = []
    for step in range(1, ranks):
        to = (rank + step) % ranks
        copies.append(send(window(acc, base + to * piece, piece), zrecv.at[step - 1], (space, to)))
    for copy in copies:
        copy.wait()
    own = base + rank * piece
    total = acc[pl.ds(pl.multiple_of(own, 8), piece), :]
    for step in range(1, ranks):
        total = total + zrecv[step - 1]
    for bit in range(doublings):
        spot = ranks - 1 + 2 * bit
        zrecv[spot] = total
        send(zrecv.at[spot], zrecv.at[spot + 1], (across(halvings + bit), rank)).wait()
        total = total + zrecv[spot + 1]
    out_ref[pl.ds(pl.multiple_of(own, 8), piece), :] = total
    copies = []
    for step in range(1, ranks):
        to = (rank + step) % ranks
        copies.append(send(window(out_ref, own, piece), window(out_ref, own, piece), (space, to)))
    for copy in copies:
        copy.wait()
    for bit in reversed(range(halvings)):
        send(window(out_ref, base, size), window(out_ref, base, size), (across(bit), rank)).wait()
        base, size = bases[bit]


def factor_tile(tile):
    n, groups, quad = 128, 16, 4
    sub = lax.broadcasted_iota(jnp.int32, (8, n), 0)
    lane = lax.broadcasted_iota(jnp.int32, (8, n), 1)
    a = [tile[8 * g : 8 * g + 8, :] for g in range(groups)]
    m = [jnp.where(lane == sub + 8 * g, 1.0, 0.0).astype(F32) for g in range(groups)]
    pivot = [jnp.ones((8, n), F32) for _ in range(groups)]

    def wide(value, row):
        return jnp.broadcast_to(value[row : row + 1, :], (8, n))

    for j in range(0, n, quad):
        g0, s = j // 8, j % 8
        cols = {g: [jnp.broadcast_to(a[g][:, j + t : j + t + 1], (8, n)) for t in range(quad)] for g in range(g0, groups)}
        small = [[wide(cols[g0][t], s + r) for t in range(quad)] for r in range(quad)]
        ra = [wide(a[g0], s + r) for r in range(quad)]
        rm = [wide(m[g0], s + r) for r in range(quad)]
        inv = []
        for r in range(quad):
            inv.append(1.0 / small[r][r])
            for q in range(r + 1, quad):
                f = small[r][q] * inv[r]
                for t in range(q, quad):
                    small[q][t] = small[q][t] - f * small[r][t]
                ra[q] = ra[q] - f * ra[r]
                rm[q] = rm[q] - f * rm[r]
        for g in range(g0, groups):
            c = cols[g]
            f = []
            for t in range(quad):
                v = c[t]
                for r in range(t):
                    v = v - f[r] * small[r][t]
                f.append(v * inv[t])
            if g == g0:
                f = [jnp.where(sub > s + quad - 1, v, 0.0) for v in f]
            for r in range(quad):
                a[g] = a[g] - f[r] * ra[r]
                m[g] = m[g] - f[r] * rm[r]
            if g == g0:
                for r in range(quad):
                    a[g] = jnp.where(sub == s + r, ra[r], a[g])
                    m[g] = jnp.where(sub == s + r, rm[r], m[g])
                    pivot[g] = jnp.where(sub == s + r, small[r][r], pivot[g])
    upper, inverse = [], []
    for g in range(groups):
        scale = 1.0 / jnp.sqrt(pivot[g])
        upper.append(jnp.where(lane >= sub + 8 * g, a[g] * scale, 0.0))
        inverse.append(m[g] * scale)
    return upper, inverse


def hdot(a, b, dims):
    return lax.dot_general(a, b, dims, precision=HIGHEST, preferred_element_type=F32)


NN = (((1,), (0,)), ((), ()))


def finish_kernel(blocks, first, gram_ref, ct_ref, chi_a, clo_a, chi_b, clo_b, r_ref, out_ref, work, inv, w, whi, wlo):
    @pl.when(pl.program_id(0) == 0)
    def _():
        at = 0
        for row in range(blocks):
            for col in range(blocks):
                if col >= row:
                    work[row, col] = gram_ref[at * 128 : (at + 1) * 128, :]
                    at += 1
                else:
                    work[row, col] = jnp.zeros((128, 128), F32)

        @pl.loop(0, blocks)
        def _(k):
            upper, inverse = factor_tile(work[k, k])
            for g in range(16):
                work[k, k, 8 * g : 8 * g + 8, :] = upper[g]
                inv[k, 8 * g : 8 * g + 8, :] = inverse[g]

            @pl.loop(k + 1, blocks)
            def _(j):
                work[k, j] = hdot(inv[k], work[k, j], NN)

            @pl.loop(k + 1, blocks)
            def _(i):
                @pl.loop(i, blocks)
                def _(j):
                    work[i, j] -= hdot(work[k, i], work[k, j], TN)

        for row in range(blocks):
            for col in range(blocks):
                r_ref[row * 128 : (row + 1) * 128, col * 128 : (col + 1) * 128] = work[row, col]
        for j in reversed(range(blocks)):
            rest = ct_ref[:, j * 128 : (j + 1) * 128]
            for i in range(j + 1, blocks):
                rest = rest - hdot(w[:, i * 128 : (i + 1) * 128], work[j, i], NT)
            w[:, j * 128 : (j + 1) * 128] = hdot(rest, inv[j], NN)
        high, low = split(w[...])
        whi[...], wlo[...] = high, low

    def product(chi_ref, clo_ref):
        out_ref[...] = mm(whi[...], chi_ref[...]) + mm(whi[...], clo_ref[...]) + mm(wlo[...], chi_ref[...])

    @pl.when(pl.program_id(0) < first)
    def _():
        product(chi_a, clo_a)

    @pl.when(pl.program_id(0) >= first)
    def _():
        product(chi_b, clo_b)


def weights(volume, upwind):
    nodes = volume.shape[1]
    zero = jnp.zeros((nodes, nodes), F32)

    def rows(odd):
        def line(blocks):
            parts = []
            for block in blocks:
                parts += [zero, block] if odd else [block, zero]
            return jnp.concatenate(parts, axis=1)

        lines = [line([volume[d].T for d in range(3)])]
        for d in range(3):
            lines.append(line([upwind[d].T if t == d else zero for t in range(3)]))
        return lines

    return jnp.concatenate(rows(0) + rows(1), axis=0)


def shards(xfactor, volume, upwind, neighbor, coeffs):
    nodes = volume.shape[1]
    ranks, spaces = lax.axis_size("rank"), lax.axis_size("space")
    rows = xfactor.shape[1]
    whole_cols = lax.all_to_all(xfactor, "rank", split_axis=1, concat_axis=0, tiled=True)
    cols, sub_rows = whole_cols.shape
    sub_elems = sub_rows // nodes
    above = shifted(whole_cols[:, sub_rows - HALO_EL * nodes :], ("space", "rank"), 1)
    rank_pos = lax.axis_index("rank")
    start = (lax.axis_index("space") * ranks + rank_pos) * sub_elems
    near = lax.dynamic_slice_in_dim(neighbor, rank_pos * sub_elems, sub_elems, 1)
    table = weights(volume, upwind)

    cand = coeffs.shape[0]
    blocks = cand // 128
    packed = blocks * (blocks + 1) // 2 * 128
    halo_pairs, pairs = HALO_EL * nodes // LANES, sub_rows // LANES
    group = 4
    width = group * 2 * LANES
    full = lambda shape: pl.BlockSpec(shape, lambda i, *_: (0,) * len(shape))

    def transport(first, count, head, body_at, prev):
        run = near[:, first : first + count]
        index = jnp.where(run >= 0, run - (start + first - HALO_EL), HALO_EL + count)
        body_pairs = count * nodes // LANES
        more = prev is not None
        dims = (cols, halo_pairs, body_pairs, body_at, group, ranks, blocks, float(rows * spaces), more)
        lanes = count * nodes
        spec = pl.BlockSpec(memory_space=pltpu.VMEM)
        return pl.pallas_call(
            functools.partial(transport_kernel, dims),
            in_specs=[pl.BlockSpec(memory_space=pltpu.SMEM)] + [spec] * (4 if more else 3),
            out_specs=[spec] * 3,
            scratch_shapes=[
                pltpu.VMEM((2, halo_pairs + body_pairs + 1, cols, LANES), BF16),
                pltpu.VMEM((2, halo_pairs + body_pairs + 1, cols, LANES), BF16),
                pltpu.VMEM((group * cols, 512), BF16),
                pltpu.VMEM((group * cols, 512), BF16),
                pltpu.VMEM(table.shape, BF16),
                pltpu.VMEM(table.shape, BF16),
            ],
            out_shape=[
                jax.ShapeDtypeStruct((cand, lanes), BF16),
                jax.ShapeDtypeStruct((cand, lanes), BF16),
                jax.ShapeDtypeStruct((packed, 128), F32),
            ],
            compiler_params=pltpu.CompilerParams(vmem_limit_bytes=VMEM_LIMIT),
            cost_estimate=pl.CostEstimate(
                flops=6 * cand * cand * lanes + 6 * cols * lanes * 1536, bytes_accessed=16 * cand * lanes, transcendentals=0
            ),
            name="transport",
        )(index, head, whole_cols, table, *([prev] if more else []))

    chi_b, clo_b, part_b = transport(HALO_EL, sub_elems - HALO_EL, whole_cols, halo_pairs, None)
    chi_a, clo_a, part = transport(0, HALO_EL, above, 0, part_b)

    bits = spaces.bit_length() - 1
    halvings = 0
    while halvings < bits and packed % (2 ** (halvings + 1) * ranks * 8) == 0:
        halvings += 1
    doublings = bits - halvings
    size = packed // 2**halvings
    sends = 2 * halvings + doublings + 2 * (ranks - 1)
    gram = pl.pallas_call(
        functools.partial(reduce_kernel, (halvings, doublings, ranks, packed)),
        out_shape=jax.ShapeDtypeStruct((packed, 128), F32),
        in_specs=[pl.BlockSpec(memory_space=pltpu.VMEM)],
        out_specs=pl.BlockSpec(memory_space=pltpu.VMEM),
        scratch_shapes=[
            pltpu.VMEM((packed, 128), F32),
            pltpu.VMEM((packed, 128), F32),
            pltpu.VMEM((ranks - 1 + 2 * doublings, size // ranks, 128), F32),
            pltpu.SemaphoreType.DMA((sends,)),
            pltpu.SemaphoreType.DMA((sends,)),
        ],
        compiler_params=pltpu.CompilerParams(collective_id=0, has_side_effects=True),
        name="reduce",
    )(part)

    out_cols = coeffs.shape[1]
    first = halo_pairs * LANES // width
    run_a = pl.BlockSpec((cand, width), lambda i: (0, jnp.minimum(i, first - 1)))
    run_b = pl.BlockSpec((cand, width), lambda i: (0, jnp.maximum(i - first, 0)))
    r_factor, new_factor = pl.pallas_call(
        functools.partial(finish_kernel, blocks, first),
        grid=(sub_rows // width,),
        in_specs=[full((packed, 128)), full((out_cols, cand)), run_a, run_a, run_b, run_b],
        out_specs=[full((cand, cand)), pl.BlockSpec((out_cols, width), lambda i: (0, i))],
        out_shape=[
            jax.ShapeDtypeStruct((cand, cand), F32),
            jax.ShapeDtypeStruct((out_cols, sub_rows), F32),
        ],
        scratch_shapes=[
            pltpu.VMEM((blocks, blocks, 128, 128), F32),
            pltpu.VMEM((blocks, 128, 128), F32),
            pltpu.VMEM((out_cols, cand), F32),
            pltpu.VMEM((out_cols, cand), BF16),
            pltpu.VMEM((out_cols, cand), BF16),
        ],
        compiler_params=pltpu.CompilerParams(vmem_limit_bytes=VMEM_LIMIT),
        name="finish",
    )(gram, coeffs.T, chi_a, clo_a, chi_b, clo_b)
    return (new_factor, r_factor)


def solution(mesh):
    return jax.shard_map(
        shards,
        mesh=mesh,
        in_specs=(P("rank", "space"), P(), P(), P(None, "space"), P()),
        out_specs=(P(None, ("space", "rank")), P()),
        check_vma=False,
    )
```
